512 devices in a mesh: stream: 16 (over y, core), cell: 32 (over x, z).
Axes of the slice: x: 4, y: 8, z: 8, core: 2. Of those that a mesh axis runs over, the one named last changes fastest.
Arguments:
- positions: float32 [16, 1024, 3, 128], P('stream', 'cell'), may hold values from 0 to 2
- strengths: float32 [16, 1024, 3, 128], P('stream', 'cell'), may hold values from -4 to 4
- fill: int32 [16, 1024], P('stream', 'cell'), may hold values from 64 to 128
- export_cells: int32 [16, 32, 32, 2], P('stream', 'cell'), may hold values from 0 to 31
- pair_local: int32 [16, 6144], P('stream', 'cell'), may hold values from 0 to 31
- pair_remote: int32 [16, 6144], P('stream', 'cell'), may hold values from 0 to 63
- pair_count: int32 [16, 32], P('stream', 'cell'), may hold values from 64 to 192
Outputs:
- new_positions: float32 [16, 1024, 3, 128], P('stream', 'cell')
- new_strengths: float32 [16, 1024, 3, 128], P('stream', 'cell')
The draws below stay inside these ranges and needn't reach their ends.
All inputs are finite; a program needn't handle non-finite values.
Results may differ from the reference program's by a relative error of at most 0.00016.
Values sent between devices are 32-bit elements; how exact they have to be, the bound alone decides.
No kernel may reach another device: no remote copies, remote signals or barrier semaphores. Data moves between devices by JAX's collectives and lax.ppermute only.
A program may use at most 64 MiB of HBM per device.

```python
import math
import jax
import jax.numpy as jnp
from jax import lax

CELLS = 32
PCELL = 128
SLOT = 2
SLABS = 16
OWNERS = 32
IMPORTS = 64
NPAIR = 192


def draw_pair_remote(key, part):
    devices = SLABS * OWNERS
    keys = jax.random.split(jax.random.fold_in(key, 11), devices)
    heads = jax.vmap(lambda single: jax.random.permutation(single, IMPORTS))(keys).astype(jnp.int32)
    tails = jax.random.randint(jax.random.fold_in(key, 12), (devices, NPAIR - IMPORTS), 0, IMPORTS, dtype=jnp.int32)
    return jnp.concatenate([heads, tails], axis=1).reshape(SLABS, OWNERS * NPAIR)


def draw_pair_count(key, part):
    level = jax.random.randint(jax.random.fold_in(key, 21), (SLABS, OWNERS), 0, 4, dtype=jnp.int32)
    counts = IMPORTS + IMPORTS * level * (level + 1) // 6
    counts = counts.at[0, 0].set(NPAIR)
    counts = counts.at[SLABS - 1, OWNERS - 1].set(IMPORTS)
    return counts.astype(jnp.int32)


def place_ends(drawn, stream_key, low, top_value):
    longest = drawn.shape.index(max(drawn.shape))
    spots = []
    for shift in (0, 1):
        where = [jax.random.randint(jax.random.fold_in(stream_key, axis), (), 0, length) for axis, length in enumerate(drawn.shape)]
        where[longest] = (where[longest] + shift) % drawn.shape[longest]
        spots.append(tuple(where))
    return drawn.at[spots[0]].set(low).at[spots[1]].set(top_value)


def levels(stream_key, dims, pieces, smallest, high):
    level, own = 1.0, jax.random.fold_in(stream_key, 6)
    for axis_at, shards_of in pieces:
        steps = jnp.exp(jax.random.uniform(jax.random.fold_in(own, axis_at), (shards_of,), jnp.float32, smallest / len(pieces), high / len(pieces)))
        level = level * jnp.repeat(steps, dims[axis_at] // shards_of).reshape([-1 if axis == axis_at else 1 for axis in range(len(dims))])
    return level


def noise(own_key, dims, scale, most, cuts=(), kind=jnp.bfloat16):
    array = scale * jax.random.normal(own_key, dims, jnp.float32)
    if cuts:
        array = array * levels(own_key, dims, cuts, -0.22, 0.18)
    return jnp.clip(array, -most, most).astype(kind)


def setup_inputs(seed: int = 0) -> dict:
    key_of = jax.random.split(jax.random.key(seed), 8)
    positions = jnp.clip(2.0 * jax.random.uniform(key_of[0], (SLABS, OWNERS * CELLS, 3, PCELL), jnp.float32) ** levels(key_of[0], (SLABS, OWNERS * CELLS, 3, PCELL), ((0, 16), (1, 32)), -0.2, 0.2), 0.0, 2.0)
    strengths = noise(key_of[1], (SLABS, OWNERS * CELLS, 3, PCELL), 0.3, 4.0, ((0, 16), (1, 32)), jnp.float32)
    fill = place_ends(jax.random.randint(key_of[2], (SLABS, OWNERS * CELLS), PCELL // 2, PCELL + 1), jax.random.fold_in(key_of[2], 1), PCELL // 2, PCELL).astype(jnp.int32)
    export_cells = place_ends(jax.random.randint(key_of[3], (SLABS, OWNERS, OWNERS, SLOT), 0, CELLS), jax.random.fold_in(key_of[3], 1), 0, CELLS - 1).astype(jnp.int32)
    pair_local = place_ends(jax.random.randint(key_of[4], (SLABS, OWNERS * NPAIR), 0, CELLS), jax.random.fold_in(key_of[4], 1), 0, CELLS - 1).astype(jnp.int32)
    pair_remote = draw_pair_remote(jax.random.fold_in(key_of[7], 71), 0)
    pair_count = draw_pair_count(jax.random.fold_in(key_of[7], 71), 0)
    return {"positions": positions, "strengths": strengths, "fill": fill, "export_cells": export_cells, "pair_local": pair_local, "pair_remote": pair_remote, "pair_count": pair_count}


sigma_sq = 0.09
spread_inv = 3.125
viscous = 0.01
time_step = 0.2
kernel_scale = 1.0 / (4.0 * math.pi)

def cross_product(left, right):
    return [left[1] * right[2] - left[2] * right[1], left[2] * right[0] - left[0] * right[2], left[0] * right[1] - left[1] * right[0]]

def pair_terms(first, second, both):
    here_pos = [first[:, k, :, None] for k in range(3)]
    there_pos = [second[:, k, None, :] for k in range(3)]
    here_str = [first[:, 3 + k, :, None] for k in range(3)]
    there_str = [second[:, 3 + k, None, :] for k in range(3)]
    here_mask = first[:, 6, :, None]
    there_mask = second[:, 6, None, :]
    sep = [here_pos[k] - there_pos[k] for k in range(3)]
    dist = sep[0] * sep[0] + sep[1] * sep[1] + sep[2] * sep[2]
    soft = dist + sigma_sq
    inverse = lax.rsqrt(soft)
    cubic = inverse * inverse * inverse
    quintic = cubic / soft
    smooth = jnp.exp(-spread_inv * dist)
    cross_there = cross_product(sep, there_str)
    twist = cross_product(here_str, there_str)
    dot_here = here_str[0] * sep[0] + here_str[1] * sep[1] + here_str[2] * sep[2]
    weight_there = there_mask * smooth
    rows = [-kernel_scale * lax.optimization_barrier(jnp.sum(cubic * cross_there[k], axis=-1)) for k in range(3)]
    rows += [-kernel_scale * lax.optimization_barrier(jnp.sum(cubic * twist[k] - 3.0 * quintic * dot_here * cross_there[k], axis=-1)) + viscous * lax.optimization_barrier(jnp.sum(weight_there * (there_str[k] - here_str[k]), axis=-1)) for k in range(3)]
    result_here = jnp.stack(rows, axis=1)
    if not both:
        return (result_here, None)
    cross_here = cross_product(sep, here_str)
    dot_there = there_str[0] * sep[0] + there_str[1] * sep[1] + there_str[2] * sep[2]
    weight_here = here_mask * smooth
    rows = [kernel_scale * lax.optimization_barrier(jnp.sum(cubic * cross_here[k], axis=-2)) for k in range(3)]
    rows += [-kernel_scale * lax.optimization_barrier(jnp.sum(-cubic * twist[k] - 3.0 * quintic * dot_there * cross_here[k], axis=-2)) + viscous * lax.optimization_barrier(jnp.sum(weight_here * (here_str[k] - there_str[k]), axis=-2)) for k in range(3)]
    return (result_here, jnp.stack(rows, axis=1))

def rate(places, vortices, mask, first_ids, second_ids, live):
    packed = jnp.concatenate([places, vortices * mask[:, None, :], mask[:, None, :]], axis=1)
    total = packed.shape[0]
    blocks = packed.reshape(total // 8, 8, 7, PCELL)
    own = lax.map(lambda block: pair_terms(block, block, False)[0], blocks).reshape(total, 6, PCELL)

    def advance(acc, item):
        ids_here, ids_there, alive = item
        near, far = pair_terms(packed[ids_here], packed[ids_there], True)
        acc = acc.at[ids_here].add(near * alive[:, None, None])
        acc = acc.at[ids_there].add(far * alive[:, None, None])
        return (acc, None)
    batch = 128
    own, _ = lax.scan(advance, own, (first_ids.reshape(-1, batch), second_ids.reshape(-1, batch), live.reshape(-1, batch)))
    return own * mask[:, None, :]

def reference(positions, strengths, fill, export_cells, pair_local, pair_remote, pair_count):
    per_slab = OWNERS * CELLS
    total = SLABS * per_slab
    slots = jnp.arange(PCELL, dtype=jnp.int32)
    mask = (slots[None, None, :] < fill[:, :, None]).astype(jnp.float32).reshape(total, PCELL)
    every = jnp.arange(total, dtype=jnp.int32)
    stream_here = every[per_slab:]
    stream_there = every[:total - per_slab]
    slab_ids = jnp.arange(SLABS, dtype=jnp.int32)[:, None]
    column = jnp.arange(OWNERS * NPAIR, dtype=jnp.int32)[None, :]
    owner_ids = column // NPAIR
    position = column % NPAIR
    sender = pair_remote // SLOT
    within = pair_remote % SLOT
    listed = export_cells[slab_ids, sender, owner_ids, within]
    remote_here = (slab_ids * per_slab + owner_ids * CELLS + pair_local).astype(jnp.int32).reshape(-1)
    remote_there = (slab_ids * per_slab + sender * CELLS + listed).astype(jnp.int32).reshape(-1)
    remote_live = (position < pair_count[slab_ids, owner_ids]).astype(jnp.float32).reshape(-1)
    count_all = stream_here.shape[0] + remote_here.shape[0]
    padding = -count_all % 128
    first_ids = jnp.concatenate([stream_here, remote_here, jnp.zeros((padding,), jnp.int32)]).astype(jnp.int32)
    second_ids = jnp.concatenate([stream_there, remote_there, jnp.zeros((padding,), jnp.int32)]).astype(jnp.int32)
    live = jnp.concatenate([jnp.ones((stream_here.shape[0],), jnp.float32), remote_live, jnp.zeros((padding,), jnp.float32)])
    places = positions.reshape(total, 3, PCELL)
    vortices = strengths.reshape(total, 3, PCELL)
    first = rate(places, vortices, mask, first_ids, second_ids, live)
    mid_places = places + time_step * first[:, 0:3]
    mid_vortices = vortices + time_step * first[:, 3:6]
    second = rate(mid_places, mid_vortices, mask, first_ids, second_ids, live)
    new_places = places + 0.5 * time_step * (first[:, 0:3] + second[:, 0:3])
    new_vortices = vortices + 0.5 * time_step * (first[:, 3:6] + second[:, 3:6])
    return (new_places.reshape(positions.shape), new_vortices.reshape(strengths.shape))
```

```python
import math

import jax
import jax.numpy as jnp
from jax import lax
from jax.experimental import pallas as pl
from jax.experimental.pallas import tpu as pltpu
from jax.sharding import PartitionSpec as P

sigma_sq = 0.09
spread_inv = 3.125
viscous = 0.01
time_step = 0.2
kernel_scale = 1.0 / (4.0 * math.pi)
smooth_rate = -spread_inv * math.log2(math.e)
smooth_scale = viscous * math.exp(spread_inv * sigma_sq)

f32 = jnp.float32
bf16 = jnp.bfloat16
MOMENTS = 48
NN = (((1,), (0,)), ((), ()))
NT = (((1,), (1,)), ((), ()))


def shifted(value, axis, steps):
    count = lax.axis_size(axis)
    leading, last = (max(0, -steps), min(count, count - steps))
    return lax.ppermute(value, axis, [(source, source + steps) for source in range(leading, last)])


def cross_rows(x, a):
    return [
        x[1] * a[2] - x[2] * a[1],
        x[2] * a[0] - x[0] * a[2],
        x[0] * a[1] - x[1] * a[0],
    ]


def rows_of(tile, first, count=3):
    return [tile[first + k : first + k + 1] for k in range(count)]


def split3(value):
    high = value.astype(bf16)
    rest = value - high.astype(f32)
    middle = rest.astype(bf16)
    low = (rest - middle.astype(f32)).astype(bf16)
    return high, middle, low


def split2(value):
    high = value.astype(bf16)
    return high, (value - high.astype(f32)).astype(bf16)


def features(tile):
    x, a = rows_of(tile, 0), rows_of(tile, 3)
    base = jnp.concatenate([tile[3:6]] + cross_rows(x, a) + [tile[6:8]], axis=0)
    full = jnp.concatenate([base, x[0] * base, x[1] * base, x[2] * base], axis=0)
    wide = jnp.concatenate(split3(full), axis=0)
    parts = [part.astype(f32) for part in split3(base)]
    narrow = jnp.concatenate(parts + [jnp.zeros((8, 128), f32)], axis=0).astype(bf16)
    return wide, narrow


def columns(tile):
    flipped = jnp.concatenate([tile] * 16, axis=0).T
    return [jnp.broadcast_to(flipped[:, k : k + 1], (128, 128)) for k in range(3)]


def weights(cols, tile):
    d = [cols[k] - tile[k : k + 1] for k in range(3)]
    soft = d[0] * d[0] + d[1] * d[1] + d[2] * d[2] + sigma_sq
    inverse = lax.rsqrt(soft)
    square = inverse * inverse
    cubic = square * inverse
    quintic = cubic * square
    smooth = jnp.exp2(soft * smooth_rate).astype(bf16)
    return split2(quintic), split2(cubic), smooth


def moments(wide, narrow, mats, dims):
    (qh, ql), (ch, cl), smooth = mats
    side = 1 if dims is NT else 0

    def dot(left, right):
        return lax.dot_general(left, right, dims, preferred_element_type=f32)

    out_q = dot(jnp.concatenate([wide, wide], axis=1), jnp.concatenate([qh, ql], axis=side))
    out_c = dot(jnp.concatenate([narrow, narrow], axis=1), jnp.concatenate([ch, cl], axis=side))
    out_s = dot(narrow, smooth)
    return jnp.concatenate(
        [
            out_q[0:32] + out_q[32:64] + out_q[64:96],
            out_c[0:8] + out_c[8:16] + out_c[16:24],
            out_s[0:8] + out_s[8:16] + out_s[16:24],
        ],
        axis=0,
    )


def credit(tile, mom):
    x, a = rows_of(tile, 0), rows_of(tile, 3)
    dot = a[0] * x[0] + a[1] * x[1] + a[2] * x[2]
    mixed = dot * mom[0:8] - a[0] * mom[8:16] - a[1] * mom[16:24] - a[2] * mom[24:32]
    turn = cross_rows(x, rows_of(mixed, 0))
    stretch = [turn[k] - mixed[3 + k : 4 + k] for k in range(3)]
    drift = cross_rows(x, rows_of(mom, 32))
    twist = cross_rows(a, rows_of(mom, 32))
    rows = [-kernel_scale * (drift[k] - mom[35 + k : 36 + k]) for k in range(3)]
    rows += [
        -kernel_scale * (twist[k] - 3.0 * stretch[k])
        + smooth_scale * (mom[40 + k : 41 + k] - a[k] * mom[46:47])
        for k in range(3)
    ]
    return jnp.concatenate(rows + [jnp.zeros((2, 128), f32)], axis=0)


def unrolled(count, step, body):
    def trip(t, carry):
        for u in range(step):
            body(t * step + u)
        return carry

    lax.fori_loop(0, count // step, trip, 0)


def pack_kernel(fill, exports, places, vortices, cells_ref, sent_ref):
    lane = lax.broadcasted_iota(jnp.int32, (1, 128), 1)
    for c in range(cells_ref.shape[0]):
        mask = (lane < fill[c]).astype(f32)
        rows = [places[k, c : c + 1] - 1.0 for k in range(3)]
        rows += [vortices[k, c : c + 1] * mask for k in range(3)]
        cells_ref[c] = jnp.concatenate(rows + [mask, jnp.zeros((1, 128), f32)], axis=0)

    def send(n):
        sent_ref[n] = cells_ref[exports[n]]

    unrolled(sent_ref.shape[0], 8, send)


def stream_kernel(cells_ref, above_ref, near_ref, far_ref):
    def pair(c):
        here, there = cells_ref[c], above_ref[c]
        mats = weights(columns(here), there)
        near_ref[c] = credit(here, moments(*features(there), mats, NT))
        far_ref[c] = credit(there, moments(*features(here), mats, NN))

    unrolled(cells_ref.shape[0], 4, pair)


def self_kernel(cells_ref, own_ref):
    def cell(c):
        here = cells_ref[c]
        own_ref[c] = credit(here, moments(*features(here), weights(columns(here), here), NN))

    unrolled(cells_ref.shape[0], 4, cell)


def remote_kernel(
    here_ids, there_ids, count, cells_ref, got_ref, near_ref, far_ref,
    cols, wide_here, narrow_here, wide_there, narrow_there, mom_here, mom_there,
):
    cells, imports = cells_ref.shape[0], got_ref.shape[0]
    blank = jnp.zeros((MOMENTS, 128), f32)

    def prepare_here(c):
        tile = cells_ref[c]
        wide_here[c], narrow_here[c] = features(tile)
        for k, col in enumerate(columns(tile)):
            cols[c, k] = col
        mom_here[c] = blank

    unrolled(cells, 4, prepare_here)

    def prepare_there(c):
        wide_there[c], narrow_there[c] = features(got_ref[c])
        mom_there[c] = blank

    unrolled(imports, 4, prepare_there)

    def pair(n):
        c, b = here_ids[n], there_ids[n]
        keep = jnp.minimum(b, imports - 1)
        own = jnp.minimum(c, cells - 1)
        mats = weights([cols[own, k] for k in range(3)], got_ref[keep])
        mom_here[c] += moments(wide_there[keep], narrow_there[keep], mats, NT)
        mom_there[b] += moments(wide_here[own], narrow_here[own], mats, NN)

    def trip(t, carry):
        for u in range(4):
            pair(t * 4 + u)
        return carry

    lax.fori_loop(0, (count[0] + 3) // 4, trip, 0)

    def finish_here(c):
        near_ref[c] = credit(cells_ref[c], mom_here[c])

    unrolled(cells, 4, finish_here)

    def finish_there(c):
        far_ref[c] = credit(got_ref[c], mom_there[c])

    unrolled(imports, 4, finish_there)


def gather_rates(exports, cells_ref, parts, back_ref, total_ref):
    total_ref[...] = parts[0][...] + parts[1][...] + parts[2][...] + parts[3][...]

    def add(n):
        total_ref[exports[n]] += back_ref[n]

    unrolled(back_ref.shape[0], 8, add)
    total_ref[...] = total_ref[...] * cells_ref[:, 6:7, :]


def middle_kernel(exports, cells_ref, own, near, remote, below, back_ref, first_ref, mid_ref, sent_ref):
    gather_rates(exports, cells_ref, (own, near, remote, below), back_ref, first_ref)
    mid_ref[...] = cells_ref[...] + time_step * first_ref[...]

    def send(n):
        sent_ref[n] = mid_ref[exports[n]]

    unrolled(sent_ref.shape[0], 8, send)


def last_kernel(
    exports, cells_ref, own, near, remote, below, back_ref, first_ref, places, vortices,
    new_places, new_vortices, total_ref,
):
    gather_rates(exports, cells_ref, (own, near, remote, below), back_ref, total_ref)
    half = 0.5 * time_step
    for c in range(cells_ref.shape[0]):
        change = half * (first_ref[c] + total_ref[c])
        for k in range(3):
            new_places[k, c : c + 1] = places[k, c : c + 1] + change[k : k + 1]
            new_vortices[k, c : c + 1] = vortices[k, c : c + 1] + change[3 + k : 4 + k]


def call(body, scalars, arrays, outs, scratch=(), name=None):
    whole = pl.BlockSpec(memory_space=pltpu.VMEM)
    single = len(outs) == 1
    shapes = [jax.ShapeDtypeStruct(shape, f32) for shape in outs]
    return pl.pallas_call(
        body,
        grid_spec=pltpu.PrefetchScalarGridSpec(
            num_scalar_prefetch=len(scalars),
            grid=(),
            in_specs=[whole] * len(arrays),
            out_specs=whole if single else [whole] * len(outs),
            scratch_shapes=list(scratch),
        ),
        out_shape=shapes[0] if single else shapes,
        compiler_params=pltpu.CompilerParams(vmem_limit_bytes=40 << 20),
        name=name,
    )(*scalars, *arrays)


def local(positions, strengths, fill, export_cells, pair_local, pair_remote, pair_count):
    places = jnp.transpose(positions[0], (1, 0, 2))
    vortices = jnp.transpose(strengths[0], (1, 0, 2))
    cells = places.shape[1]
    owners, per_owner = export_cells.shape[2:]
    imports = owners * per_owner
    exports = export_cells[0, 0].reshape(-1)
    slots = pair_local.shape[1]
    count = pair_count[0]
    alive = jnp.arange(slots, dtype=jnp.int32) < count
    here_ids = jnp.where(alive, pair_local[0], cells)
    there_ids = jnp.where(alive, pair_remote[0], imports)
    tile, traded = (cells, 8, 128), (imports, 8, 128)

    def exchange(value):
        value = value.reshape(owners, per_owner, 8, 128)
        value = lax.all_to_all(value, "cell", split_axis=0, concat_axis=0, tiled=True)
        return value.reshape(traded)

    def rates(packed, sent):
        above = shifted(packed, "stream", 1)
        got = exchange(sent)
        near, far = call(stream_kernel, (), (packed, above), (tile, tile), name="stream")
        below = shifted(far, "stream", -1)
        got, near = lax.optimization_barrier((got, near))
        remote, back = call(
            remote_kernel, (here_ids, there_ids, count), (packed, got), (tile, traded),
            (
                pltpu.VMEM((cells, 3, 128, 128), f32),
                pltpu.VMEM((cells, 96, 128), bf16),
                pltpu.VMEM((cells, 32, 128), bf16),
                pltpu.VMEM((imports, 96, 128), bf16),
                pltpu.VMEM((imports, 32, 128), bf16),
                pltpu.VMEM((cells + 1, MOMENTS, 128), f32),
                pltpu.VMEM((imports + 1, MOMENTS, 128), f32),
            ),
            name="remote",
        )
        late, _ = lax.optimization_barrier((packed, back))
        back = exchange(back)
        own = call(self_kernel, (), (late,), (tile,), name="own")
        return own, near, remote, below, back

    packed, sent = call(pack_kernel, (fill[0], exports), (places, vortices), (tile, traded), name="pack")
    first, middle, sent = call(
        middle_kernel, (exports,), (packed, *rates(packed, sent)), (tile, tile, traded), name="middle"
    )
    shape = places.shape
    new_places, new_vortices = call(
        last_kernel, (exports,), (middle, *rates(middle, sent), first, places, vortices), (shape, shape),
        (pltpu.VMEM(tile, f32),), name="last",
    )
    return (jnp.transpose(new_places, (1, 0, 2))[None], jnp.transpose(new_vortices, (1, 0, 2))[None])


def solution(mesh):
    in_specs = (
        P("stream", "cell", None, None),
        P("stream", "cell", None, None),
        P("stream", "cell"),
        P("stream", "cell", None, None),
        P("stream", "cell"),
        P("stream", "cell"),
        P("stream", "cell"),
    )
    out_specs = (P("stream", "cell", None, None), P("stream", "cell", None, None))
    return jax.shard_map(local, mesh=mesh, in_specs=in_specs, out_specs=out_specs, check_vma=False)
```

```python
import math

import jax
import jax.numpy as jnp
from jax import lax
from jax.experimental import pallas as pl
from jax.experimental.pallas import tpu as pltpu
from jax.sharding import PartitionSpec as P

sigma_sq = 0.09
spread_inv = 3.125
viscous = 0.01
time_step = 0.2
kernel_scale = 1.0 / (4.0 * math.pi)
smooth_rate = -spread_inv * math.log2(math.e)
smooth_scale = viscous * math.exp(spread_inv * sigma_sq)

f32 = jnp.float32
bf16 = jnp.bfloat16
MOMENTS = 48
NN = (((1,), (0,)), ((), ()))
NT = (((1,), (1,)), ((), ()))


def shifted(value, axis, steps):
    count = lax.axis_size(axis)
    leading, last = (max(0, -steps), min(count, count - steps))
    return lax.ppermute(value, axis, [(source, source + steps) for source in range(leading, last)])


def cross_rows(x, a):
    return [
        x[1] * a[2] - x[2] * a[1],
        x[2] * a[0] - x[0] * a[2],
        x[0] * a[1] - x[1] * a[0],
    ]


def dot_rows(x, a):
    return x[0] * a[0] + x[1] * a[1] + x[2] * a[2]


def unrolled(count, step, body):
    def trip(t, carry):
        for u in range(step):
            body(t * step + u)
        return carry

    lax.fori_loop(0, count // step, trip, 0)


def split2(value):
    high = value.astype(bf16)
    return high, (value - high.astype(f32)).astype(bf16)


def fill_bases(tiles, bases):
    bases[...] = tiles[...]

    def group(t):
        x, a = [[tiles[pl.ds(t * 64 + first + k, 8, stride=8), :] for k in range(3)] for first in (0, 3)]
        for k, row in enumerate(cross_rows(x, a)):
            bases[pl.ds(t * 64 + k, 8, stride=8), :] = row

    unrolled(tiles.shape[0] // 64, 2, group)


def features(tile, base):
    x = [tile[k : k + 1] for k in range(3)]
    parts = []
    for scale in (None, x[0], x[1], x[2], dot_rows(x, x)):
        value = base if scale is None else scale * base
        high = value.astype(bf16).astype(f32)
        rest = value - high
        middle = rest.astype(bf16).astype(f32)
        parts += [high, middle, rest - middle]
        if scale is None:
            parts.append(jnp.zeros((8, 128), f32))
    return jnp.concatenate(parts, axis=0).astype(bf16)


def columns(tile):
    flipped = jnp.concatenate([tile] * 16, axis=0).T
    return [jnp.broadcast_to(flipped[:, k : k + 1], (128, 128)) for k in range(3)]


def weights(cols, tile):
    d = [cols[k] - tile[k : k + 1] for k in range(3)]
    soft = dot_rows(d, d) + sigma_sq
    inverse = lax.rsqrt(soft)
    square = inverse * inverse
    quintic = square * square * inverse
    smooth = jnp.exp2(soft * smooth_rate)
    return split2(quintic), split2(smooth)


def moments(wide, mats, dims):
    side = 1 if dims is NT else 0
    twice = jnp.concatenate([wide, wide], axis=1)
    quintic, smooth = [jnp.concatenate(parts, axis=side) for parts in mats]
    q = lax.dot_general(twice, quintic, dims, preferred_element_type=f32)
    s = lax.dot_general(twice[0:32], smooth, dims, preferred_element_type=f32)
    starts = (0, 32, 56, 80, 104)
    tiles = [q[k : k + 8] + q[k + 8 : k + 16] + q[k + 16 : k + 24] for k in starts]
    return tiles + [s[0:8] + s[8:16] + s[16:24]]


def put(target, c, tiles, add=False):
    for k, tile in enumerate(tiles):
        rows = pl.ds(pl.multiple_of(c * MOMENTS + 8 * k, 8), 8)
        target[rows, :] = target[rows, :] + tile if add else tile


def credits(tiles, moment, out):
    def group(t):
        def cell_rows(first, count=3):
            return [tiles[pl.ds(t * 64 + first + k, 8, stride=8), :] for k in range(count)]

        def sums(which, first, count=3):
            at = t * 8 * MOMENTS + which * 8 + first
            return [moment[pl.ds(at + k, 8, stride=MOMENTS), :] for k in range(count)]

        x, a = cell_rows(0), cell_rows(3)
        spin, norm = dot_rows(a, x), dot_rows(x, x) + sigma_sq
        twice = [2.0 * x[k] for k in range(3)]
        parts = [sums(which, 0, 6) for which in range(5)]
        mixed = [
            spin * parts[0][r] - a[0] * parts[1][r] - a[1] * parts[2][r] - a[2] * parts[3][r] for r in range(6)
        ]
        cubic = [
            norm * parts[0][r] + parts[4][r]
            - twice[0] * parts[1][r] - twice[1] * parts[2][r] - twice[2] * parts[3][r]
            for r in range(6)
        ]
        turn, drift = cross_rows(x, mixed[3:6]), cross_rows(x, cubic[3:6])
        twist = cross_rows(a, cubic[3:6])
        spread, total = sums(5, 3), sums(5, 6, 1)[0]
        for k in range(3):
            out[pl.ds(t * 64 + k, 8, stride=8), :] = -kernel_scale * (drift[k] - cubic[k])
            out[pl.ds(t * 64 + 3 + k, 8, stride=8), :] = -kernel_scale * (
                twist[k] - 3.0 * (turn[k] - mixed[k])
            ) + smooth_scale * (spread[k] - a[k] * total)
        for k in (6, 7):
            out[pl.ds(t * 64 + k, 8, stride=8), :] = jnp.zeros((8, 128), f32)

    unrolled(tiles.shape[0] // 64, 2, group)


def tile_rows(ref, c):
    return ref[pl.ds(pl.multiple_of(c * 8, 8), 8), :]


def pack_kernel(fill, exports, places, vortices, cells_ref, sent_ref):
    lane = lax.broadcasted_iota(jnp.int32, (1, 128), 1)
    for c in range(cells_ref.shape[0] // 8):
        mask = (lane < fill[c]).astype(f32)
        rows = [places[k, c : c + 1] - 1.0 for k in range(3)]
        rows += [vortices[k, c : c + 1] * mask for k in range(3)]
        cells_ref[8 * c : 8 * c + 8] = jnp.concatenate(rows + [mask, jnp.zeros((1, 128), f32)], axis=0)
    send(exports, cells_ref, sent_ref)


def send(exports, cells_ref, sent_ref):
    def one(n):
        sent_ref[pl.ds(pl.multiple_of(n * 8, 8), 8), :] = tile_rows(cells_ref, exports[n])

    unrolled(sent_ref.shape[0] // 8, 8, one)


def near_kernel(
    cells_ref, above_ref, near_ref, far_ref, wide_ref, cols_out, base_here, base_there, mom_near, mom_far, kept, sem
):
    fill_bases(cells_ref, base_here)
    fill_bases(above_ref, base_there)

    def cell(c):
        here, there = tile_rows(cells_ref, c), tile_rows(above_ref, c)
        wide = features(here, tile_rows(base_here, c))
        wide_there = features(there, tile_rows(base_there, c))
        cols = columns(here)
        joint = weights(cols, there)
        near = moments(wide_there, joint, NT)
        far = moments(wide, joint, NN)
        own = moments(wide, weights(cols, here), NN)
        wide_ref[c] = wide
        for k in range(3):
            kept[c, k] = cols[k]
        put(mom_far, c, far)
        put(mom_near, c, [p + q for p, q in zip(near, own)])

    unrolled(wide_ref.shape[0], 4, cell)
    copy = pltpu.make_async_copy(kept, cols_out, sem)
    copy.start()
    credits(above_ref, mom_far, far_ref)
    credits(cells_ref, mom_near, near_ref)
    copy.wait()


def far_kernel(here_ids, there_ids, count, cols_ref, wide_ref, got_ref, far_ref, wide_out, cols, sem, base, mom):
    cells, imports = cols.shape[0], wide_out.shape[0]
    copy = pltpu.make_async_copy(cols_ref, cols, sem)
    copy.start()
    fill_bases(got_ref, base)
    mom[...] = jnp.zeros(mom.shape, f32)

    def prepare(b):
        wide_out[b] = features(tile_rows(got_ref, b), tile_rows(base, b))

    unrolled(imports, 8, prepare)
    copy.wait()

    def pair(n):
        c, b = jnp.minimum(here_ids[n], cells - 1), there_ids[n]
        mats = weights([cols[c, k] for k in range(3)], tile_rows(got_ref, jnp.minimum(b, imports - 1)))
        put(mom, b, moments(wide_ref[c], mats, NN), add=True)

    pairs(count, pair)
    credits(got_ref, mom, far_ref)


def here_kernel(here_ids, there_ids, count, cols_ref, wide_ref, got_ref, cells_ref, own_ref, cols, sem, mom):
    cells, imports = cols.shape[0], wide_ref.shape[0]
    copy = pltpu.make_async_copy(cols_ref, cols, sem)
    copy.start()
    mom[...] = jnp.zeros(mom.shape, f32)
    copy.wait()

    def pair(n):
        c, b = here_ids[n], jnp.minimum(there_ids[n], imports - 1)
        cell = jnp.minimum(c, cells - 1)
        mats = weights([cols[cell, k] for k in range(3)], tile_rows(got_ref, b))
        put(mom, c, moments(wide_ref[b], mats, NT), add=True)

    pairs(count, pair)
    credits(cells_ref, mom, own_ref)


def pairs(count, pair):
    def trip(t, carry):
        for u in range(16):
            pair(t * 16 + u)
        return carry

    lax.fori_loop(0, (count[0] + 15) // 16, trip, 0)


def gather_rates(exports, cells_ref, parts, back_ref, total_ref):
    total_ref[...] = parts[0][...] + parts[1][...] + parts[2][...]

    def add(n):
        at = pl.ds(pl.multiple_of(exports[n] * 8, 8), 8)
        total_ref[at, :] = total_ref[at, :] + tile_rows(back_ref, n)

    unrolled(back_ref.shape[0] // 8, 8, add)
    for c in range(total_ref.shape[0] // 8):
        rows = slice(8 * c, 8 * c + 8)
        total_ref[rows] = total_ref[rows] * cells_ref[8 * c + 6 : 8 * c + 7]


def middle_kernel(exports, cells_ref, near, remote, below, back_ref, first_ref, mid_ref, sent_ref):
    gather_rates(exports, cells_ref, (near, remote, below), back_ref, first_ref)
    mid_ref[...] = cells_ref[...] + time_step * first_ref[...]
    send(exports, mid_ref, sent_ref)


def last_kernel(
    exports, cells_ref, near, remote, below, back_ref, first_ref, places, vortices,
    new_places, new_vortices, total_ref,
):
    gather_rates(exports, cells_ref, (near, remote, below), back_ref, total_ref)
    half = 0.5 * time_step
    for c in range(total_ref.shape[0] // 8):
        change = half * (first_ref[8 * c : 8 * c + 8] + total_ref[8 * c : 8 * c + 8])
        for k in range(3):
            new_places[k, c : c + 1] = places[k, c : c + 1] + change[k : k + 1]
            new_vortices[k, c : c + 1] = vortices[k, c : c + 1] + change[3 + k : 4 + k]


def call(body, scalars, arrays, outs, scratch=(), name=None):
    def spec(shape):
        return pl.BlockSpec(memory_space=pltpu.HBM if len(shape) == 4 else pltpu.VMEM)

    def shape(out):
        if len(out) == 4:
            return pltpu.HBM(out, f32)
        return jax.ShapeDtypeStruct(out, bf16 if len(out) == 3 and out[1] == 128 else f32)

    outs = [shape(out) for out in outs]
    arrays = [pltpu.with_memory_space_constraint(one, pltpu.HBM) if one.ndim == 4 else one for one in arrays]
    return pl.pallas_call(
        body,
        grid_spec=pltpu.PrefetchScalarGridSpec(
            num_scalar_prefetch=len(scalars),
            grid=(),
            in_specs=[spec(array.shape) for array in arrays],
            out_specs=[spec(out.shape) for out in outs],
            scratch_shapes=[pltpu.VMEM(one, f32) if isinstance(one, tuple) else one for one in scratch],
        ),
        out_shape=outs,
        compiler_params=pltpu.CompilerParams(vmem_limit_bytes=20 << 20),
        name=name,
    )(*scalars, *arrays)


def local(positions, strengths, fill, export_cells, pair_local, pair_remote, pair_count):
    places = jnp.transpose(positions[0], (1, 0, 2))
    vortices = jnp.transpose(strengths[0], (1, 0, 2))
    cells = places.shape[1]
    owners, per_owner = export_cells.shape[2:]
    imports = owners * per_owner
    exports = export_cells[0, 0].reshape(-1)
    count = pair_count[0]
    alive = jnp.arange(pair_local.shape[1], dtype=jnp.int32) < count
    here_ids = jnp.where(alive, pair_local[0], cells)
    there_ids = jnp.where(alive, pair_remote[0], imports)
    tile, traded = (cells * 8, 128), (imports * 8, 128)
    spread, done = (cells, 3, 128, 128), pltpu.SemaphoreType.DMA

    def exchange(value):
        value = value.reshape(owners, per_owner, 8, 128)
        value = lax.all_to_all(value, "cell", split_axis=0, concat_axis=0, tiled=True)
        return value.reshape(traded)

    def rates(packed, sent):
        above = shifted(packed, "stream", 1)
        got = exchange(sent)
        near, far, wide, cols = call(
            near_kernel, (), (packed, above),
            (tile, tile, (cells, 128, 128), spread),
            (tile, tile, (cells * MOMENTS, 128), (cells * MOMENTS, 128), spread, done), name="near",
        )
        below = shifted(far, "stream", -1)
        got, near = lax.optimization_barrier((got, near))
        listed = (here_ids, there_ids, count)
        back, wide_there = call(
            far_kernel, listed, (cols, wide, got), (traded, (imports, 128, 128)),
            (spread, done, traded, ((imports + 1) * MOMENTS, 128)), name="far",
        )
        returned = exchange(back)
        (remote,) = call(
            here_kernel, listed, (cols, wide_there, got, packed), (tile,),
            (spread, done, ((cells + 1) * MOMENTS, 128),), name="here",
        )
        return near, remote, below, returned

    packed, sent = call(pack_kernel, (fill[0], exports), (places, vortices), (tile, traded), name="pack")
    first, middle, sent = call(
        middle_kernel, (exports,), (packed, *rates(packed, sent)), (tile, tile, traded), name="middle"
    )
    shape = places.shape
    new_places, new_vortices = call(
        last_kernel, (exports,), (middle, *rates(middle, sent), first, places, vortices), (shape, shape),
        (tile,), name="last",
    )
    return (jnp.transpose(new_places, (1, 0, 2))[None], jnp.transpose(new_vortices, (1, 0, 2))[None])


def solution(mesh):
    in_specs = (
        P("stream", "cell", None, None),
        P("stream", "cell", None, None),
        P("stream", "cell"),
        P("stream", "cell", None, None),
        P("stream", "cell"),
        P("stream", "cell"),
        P("stream", "cell"),
    )
    out_specs = (P("stream", "cell", None, None), P("stream", "cell", None, None))
    return jax.shard_map(local, mesh=mesh, in_specs=in_specs, out_specs=out_specs, check_vma=False)
```

```python
import math

import jax
import jax.numpy as jnp
from jax import lax
from jax.experimental import pallas as pl
from jax.experimental.pallas import tpu as pltpu
from jax.sharding import PartitionSpec as P

sigma_sq = 0.09
spread_inv = 3.125
viscous = 0.01
time_step = 0.2
kernel_scale = 1.0 / (4.0 * math.pi)
smooth_rate = -spread_inv * math.log2(math.e)
smooth_scale = viscous * math.exp(spread_inv * sigma_sq)

f32 = jnp.float32
bf16 = jnp.bfloat16
MOMENTS = 48
UNROLL = 16
NN = (((1,), (0,)), ((), ()))
NT = (((1,), (1,)), ((), ()))


def shifted(value, axis, steps):
    count = lax.axis_size(axis)
    leading, last = (max(0, -steps), min(count, count - steps))
    return lax.ppermute(value, axis, [(source, source + steps) for source in range(leading, last)])


def cross_rows(x, a):
    return [
        x[1] * a[2] - x[2] * a[1],
        x[2] * a[0] - x[0] * a[2],
        x[0] * a[1] - x[1] * a[0],
    ]


def dot_rows(x, a):
    return x[0] * a[0] + x[1] * a[1] + x[2] * a[2]


def unrolled(count, step, body):
    def trip(t, carry):
        for u in range(step):
            body(t * step + u)
        return carry

    lax.fori_loop(0, count // step, trip, 0)


def split2(value):
    high = value.astype(bf16)
    return high, (value - high.astype(f32)).astype(bf16)


def fill_bases(tiles, bases):
    bases[...] = tiles[...]

    def group(t):
        x, a = [[tiles[pl.ds(t * 64 + first + k, 8, stride=8), :] for k in range(3)] for first in (0, 3)]
        for k, row in enumerate(cross_rows(x, a)):
            bases[pl.ds(t * 64 + k, 8, stride=8), :] = row

    unrolled(tiles.shape[0] // 64, 2, group)


def features(tile, base):
    x = [tile[k : k + 1] for k in range(3)]
    parts = []
    for scale in (None, x[0], x[1], x[2]):
        value = base if scale is None else scale * base
        high = value.astype(bf16).astype(f32)
        rest = value - high
        middle = rest.astype(bf16).astype(f32)
        parts += [high, middle, rest - middle]
        if scale is None:
            parts.append(jnp.zeros((8, 128), f32))
    return jnp.concatenate(parts + [jnp.zeros((8, 128), f32)], axis=0).astype(bf16)


def columns(tile):
    flipped = jnp.concatenate([tile] * 16, axis=0).T
    return [jnp.broadcast_to(flipped[:, k : k + 1], (128, 128)) for k in range(3)]


def weights(cols, tile, skip=None):
    d = [cols[k] - tile[k : k + 1] for k in range(3)]
    soft = dot_rows(d, d) + sigma_sq
    inverse = lax.rsqrt(soft)
    square = inverse * inverse
    cubic = square * inverse
    quintic = square * cubic
    smooth = jnp.exp2(soft * smooth_rate)
    if skip is not None:
        quintic, cubic, smooth = [jnp.where(skip, 0.0, value) for value in (quintic, cubic, smooth)]
    return split2(quintic), split2(cubic), (smooth.astype(bf16),)


def moments(wide, mats, dims):
    twice = jnp.concatenate([wide, wide], axis=1)
    out = []
    for parts, left in zip(mats, (twice, twice[0:32], wide[0:32])):
        right = jnp.concatenate(parts, axis=1 if dims is NT else 0) if len(parts) > 1 else parts[0]
        sums = lax.dot_general(left, right, dims, preferred_element_type=f32)
        starts = (0, 32, 56, 80) if left.shape[0] > 32 else (0,)
        out += [sums[k : k + 8] + sums[k + 8 : k + 16] + sums[k + 16 : k + 24] for k in starts]
    return out


def put(target, c, tiles, add=False):
    for k, tile in enumerate(tiles):
        rows = pl.ds(pl.multiple_of(c * MOMENTS + 8 * k, 8), 8)
        target[rows, :] = target[rows, :] + tile if add else tile


def credits(tiles, moment, out):
    def group(t):
        def cell_rows(first, count=3):
            return [tiles[pl.ds(t * 64 + first + k, 8, stride=8), :] for k in range(count)]

        def sums(which, first, count=3):
            at = t * 8 * MOMENTS + which * 8 + first
            return [moment[pl.ds(at + k, 8, stride=MOMENTS), :] for k in range(count)]

        x, a = cell_rows(0), cell_rows(3)
        spin = dot_rows(a, x)
        parts = [sums(which, 0, 6) for which in range(5)]
        mixed = [
            spin * parts[0][r] - a[0] * parts[1][r] - a[1] * parts[2][r] - a[2] * parts[3][r] for r in range(6)
        ]
        cubic = parts[4]
        turn, drift = cross_rows(x, mixed[3:6]), cross_rows(x, cubic[3:6])
        twist = cross_rows(a, cubic[3:6])
        spread, total = sums(5, 3), sums(5, 6, 1)[0]
        for k in range(3):
            out[pl.ds(t * 64 + k, 8, stride=8), :] = -kernel_scale * (drift[k] - cubic[k])
            out[pl.ds(t * 64 + 3 + k, 8, stride=8), :] = -kernel_scale * (
                twist[k] - 3.0 * (turn[k] - mixed[k])
            ) + smooth_scale * (spread[k] - a[k] * total)
        for k in (6, 7):
            out[pl.ds(t * 64 + k, 8, stride=8), :] = jnp.zeros((8, 128), f32)

    unrolled(tiles.shape[0] // 64, 2, group)


def tile_rows(ref, c):
    return ref[pl.ds(pl.multiple_of(c * 8, 8), 8), :]


def pack_kernel(fill, exports, places, vortices, cells_ref, sent_ref):
    lane = lax.broadcasted_iota(jnp.int32, (1, 128), 1)
    for c in range(cells_ref.shape[0] // 8):
        mask = (lane < fill[c]).astype(f32)
        rows = [places[k, c : c + 1] - 1.0 for k in range(3)]
        rows += [vortices[k, c : c + 1] * mask for k in range(3)]
        cells_ref[8 * c : 8 * c + 8] = jnp.concatenate(rows + [mask, jnp.zeros((1, 128), f32)], axis=0)
    send(exports, cells_ref, sent_ref)


def send(exports, cells_ref, sent_ref):
    def one(n):
        sent_ref[pl.ds(pl.multiple_of(n * 8, 8), 8), :] = tile_rows(cells_ref, exports[n])

    unrolled(sent_ref.shape[0] // 8, 8, one)


def near_kernel(
    cells_ref, above_ref, near_ref, far_ref, wide_out, cols_out,
    base_here, base_there, mom_near, mom_far, wide_here, cols_here, sems,
):
    fill_bases(cells_ref, base_here)
    fill_bases(above_ref, base_there)
    row, column = [lax.broadcasted_iota(jnp.int32, (128, 128), axis) for axis in (0, 1)]
    itself = row == column

    def cell(c):
        here, there = tile_rows(cells_ref, c), tile_rows(above_ref, c)
        wide = features(here, tile_rows(base_here, c))
        wide_there = features(there, tile_rows(base_there, c))
        cols = columns(here)
        joint = weights(cols, there)
        near = moments(wide_there, joint, NT)
        far = moments(wide, joint, NN)
        own = moments(wide, weights(cols, here, itself), NN)
        wide_here[c, 0] = wide
        for k in range(3):
            cols_here[c, k] = cols[k]
        put(mom_far, c, far)
        put(mom_near, c, [p + q for p, q in zip(near, own)])

    half = wide_here.shape[0] // 2
    copies = []
    for part in range(2):
        unrolled(half, 4, lambda c: cell(c + part * half))
        rows = pl.ds(part * half, half)
        for k, (kept, out) in enumerate(((wide_here, wide_out), (cols_here, cols_out))):
            copies.append(pltpu.make_async_copy(kept.at[rows], out.at[rows], sems.at[part, k]))
            copies[-1].start()
    credits(above_ref, mom_far, far_ref)
    credits(cells_ref, mom_near, near_ref)
    for copy in copies:
        copy.wait()


def far_kernel(
    here_ids, there_ids, count, wide_ref, cols_ref, got_ref, far_ref, wide_out,
    wide_here, cols, sems, base, mom,
):
    cells, imports = cols.shape[0], wide_out.shape[0]
    copies = [
        pltpu.make_async_copy(source, kept, sems.at[0, k])
        for k, (source, kept) in enumerate(((wide_ref, wide_here), (cols_ref, cols)))
    ]
    for copy in copies:
        copy.start()
    fill_bases(got_ref, base)
    mom[...] = jnp.zeros(mom.shape, f32)

    def prepare(b):
        wide_out[b] = features(tile_rows(got_ref, b), tile_rows(base, b))

    unrolled(imports, 8, prepare)
    for copy in copies:
        copy.wait()

    def pair(n):
        c, b = jnp.minimum(here_ids[n], cells - 1), there_ids[n]
        mats = weights([cols[c, k] for k in range(3)], tile_rows(got_ref, jnp.minimum(b, imports - 1)))
        put(mom, b, moments(wide_here[c, 0], mats, NN), add=True)

    pairs(count, pair)
    credits(got_ref, mom, far_ref)


def here_kernel(here_ids, there_ids, count, cols_ref, wide_ref, got_ref, cells_ref, own_ref, cols, sems, mom):
    cells, imports = cols.shape[0], wide_ref.shape[0]
    copy = pltpu.make_async_copy(cols_ref, cols, sems.at[0, 0])
    copy.start()
    mom[...] = jnp.zeros(mom.shape, f32)
    copy.wait()

    def pair(n):
        c, b = here_ids[n], jnp.minimum(there_ids[n], imports - 1)
        cell = jnp.minimum(c, cells - 1)
        mats = weights([cols[cell, k] for k in range(3)], tile_rows(got_ref, b))
        put(mom, c, moments(wide_ref[b], mats, NT), add=True)

    pairs(count, pair)
    credits(cells_ref, mom, own_ref)


def pairs(count, pair):
    def trip(t, carry):
        for u in range(UNROLL):
            pair(t * UNROLL + u)
        return carry

    lax.fori_loop(0, (count[0] + UNROLL - 1) // UNROLL, trip, 0)


def gather_rates(exports, cells_ref, parts, back_ref, total_ref):
    total_ref[...] = parts[0][...] + parts[1][...] + parts[2][...]

    def add(n):
        at = pl.ds(pl.multiple_of(exports[n] * 8, 8), 8)
        total_ref[at, :] = total_ref[at, :] + tile_rows(back_ref, n)

    unrolled(back_ref.shape[0] // 8, 8, add)
    for c in range(total_ref.shape[0] // 8):
        rows = slice(8 * c, 8 * c + 8)
        total_ref[rows] = total_ref[rows] * cells_ref[8 * c + 6 : 8 * c + 7]


def middle_kernel(exports, cells_ref, near, remote, below, back_ref, first_ref, mid_ref, sent_ref):
    gather_rates(exports, cells_ref, (near, remote, below), back_ref, first_ref)
    mid_ref[...] = cells_ref[...] + time_step * first_ref[...]
    send(exports, mid_ref, sent_ref)


def last_kernel(
    exports, cells_ref, near, remote, below, back_ref, first_ref, places, vortices,
    new_places, new_vortices, total_ref,
):
    gather_rates(exports, cells_ref, (near, remote, below), back_ref, total_ref)
    half = 0.5 * time_step
    for c in range(total_ref.shape[0] // 8):
        change = half * (first_ref[8 * c : 8 * c + 8] + total_ref[8 * c : 8 * c + 8])
        for k in range(3):
            new_places[k, c : c + 1] = places[k, c : c + 1] + change[k : k + 1]
            new_vortices[k, c : c + 1] = vortices[k, c : c + 1] + change[3 + k : 4 + k]


def call(body, scalars, arrays, outs, scratch=(), name=None):
    def spec(one):
        if len(one.shape) == 4:
            return pl.BlockSpec(memory_space=pltpu.HBM)
        zeros = (0,) * len(one.shape)
        return pl.BlockSpec(one.shape, lambda i, *_: zeros, pipeline_mode=pl.Buffered(1))

    outs = [out if len(out) == 2 and isinstance(out[0], tuple) else (out, f32) for out in outs]
    outs = [pltpu.HBM(*out) if len(out[0]) == 4 else jax.ShapeDtypeStruct(*out) for out in outs]
    arrays = [pltpu.with_memory_space_constraint(one, pltpu.HBM) if one.ndim == 4 else one for one in arrays]
    return pl.pallas_call(
        body,
        grid_spec=pltpu.PrefetchScalarGridSpec(
            num_scalar_prefetch=len(scalars),
            grid=(1,),
            in_specs=[spec(array) for array in arrays],
            out_specs=[spec(out) for out in outs],
            scratch_shapes=[pltpu.VMEM(one, f32) if isinstance(one, tuple) else one for one in scratch],
        ),
        out_shape=outs,
        compiler_params=pltpu.CompilerParams(vmem_limit_bytes=20 << 20),
        cost_estimate=pl.CostEstimate(flops=10**10 if name in ("near", "far", "here") else 10**8, bytes_accessed=10**6, transcendentals=0),
        name=name,
    )(*scalars, *arrays)


def local(positions, strengths, fill, export_cells, pair_local, pair_remote, pair_count):
    places = jnp.transpose(positions[0], (1, 0, 2))
    vortices = jnp.transpose(strengths[0], (1, 0, 2))
    cells = places.shape[1]
    owners, per_owner = export_cells.shape[2:]
    imports = owners * per_owner
    exports = export_cells[0, 0].reshape(-1)
    count = pair_count[0]
    alive = jnp.arange(pair_local.shape[1], dtype=jnp.int32) < count
    here_ids = jnp.where(alive, pair_local[0], cells)
    there_ids = jnp.where(alive, pair_remote[0], imports)
    tile, traded = (cells * 8, 128), (imports * 8, 128)
    spread, gathered = (cells, 3, 128, 128), ((cells + 1) * MOMENTS, 128)
    kept, sems = pltpu.VMEM((cells, 1, 112, 128), bf16), pltpu.SemaphoreType.DMA((2, 2))

    def exchange(value):
        value = value.reshape(owners, per_owner, 8, 128)
        value = lax.all_to_all(value, "cell", split_axis=0, concat_axis=0, tiled=True)
        return value.reshape(traded)

    def rates(packed, sent):
        above = shifted(packed, "stream", 1)
        got = exchange(sent)
        near, far, wide, cols = call(
            near_kernel, (), (packed, above), (tile, tile, ((cells, 1, 112, 128), bf16), spread),
            (tile, tile, (cells * MOMENTS, 128), (cells * MOMENTS, 128), kept, spread, sems), name="near",
        )
        below = shifted(far, "stream", -1)
        got, near = lax.optimization_barrier((got, near))
        listed = (here_ids, there_ids, count)
        back, wide_there = call(
            far_kernel, listed, (wide, cols, got), (traded, ((imports, 112, 128), bf16)),
            (kept, spread, sems, traded, ((imports + 1) * MOMENTS, 128)), name="far",
        )
        returned = exchange(back)
        (remote,) = call(
            here_kernel, listed, (cols, wide_there, got, packed), (tile,),
            (spread, sems, gathered), name="here",
        )
        return near, remote, below, returned

    packed, sent = call(pack_kernel, (fill[0], exports), (places, vortices), (tile, traded), name="pack")
    first, middle, sent = call(
        middle_kernel, (exports,), (packed, *rates(packed, sent)), (tile, tile, traded), name="middle"
    )
    shape = places.shape
    new_places, new_vortices = call(
        last_kernel, (exports,), (middle, *rates(middle, sent), first, places, vortices), (shape, shape),
        (tile,), name="last",
    )
    return (jnp.transpose(new_places, (1, 0, 2))[None], jnp.transpose(new_vortices, (1, 0, 2))[None])


def solution(mesh):
    in_specs = (
        P("stream", "cell", None, None),
        P("stream", "cell", None, None),
        P("stream", "cell"),
        P("stream", "cell", None, None),
        P("stream", "cell"),
        P("stream", "cell"),
        P("stream", "cell"),
    )
    out_specs = (P("stream", "cell", None, None), P("stream", "cell", None, None))
    return jax.shard_map(local, mesh=mesh, in_specs=in_specs, out_specs=out_specs, check_vma=False)
```

```python
import math

import jax
import jax.numpy as jnp
from jax import lax
from jax.experimental import pallas as pl
from jax.experimental.pallas import tpu as pltpu
from jax.sharding import PartitionSpec as P

sigma_sq = 0.09
spread_inv = 3.125
viscous = 0.01
time_step = 0.2
kernel_scale = 1.0 / (4.0 * math.pi)
smooth_rate = -spread_inv * math.log2(math.e)
smooth_scale = viscous * math.exp(spread_inv * sigma_sq)

f32 = jnp.float32
bf16 = jnp.bfloat16
MOMENTS = 48
UNROLL = 16
HIDDEN = 8
NN = (((1,), (0,)), ((), ()))
NT = (((1,), (1,)), ((), ()))


def shifted(value, axis, steps):
    count = lax.axis_size(axis)
    leading, last = (max(0, -steps), min(count, count - steps))
    return lax.ppermute(value, axis, [(source, source + steps) for source in range(leading, last)])


def cross_rows(x, a):
    return [
        x[1] * a[2] - x[2] * a[1],
        x[2] * a[0] - x[0] * a[2],
        x[0] * a[1] - x[1] * a[0],
    ]


def dot_rows(x, a):
    return x[0] * a[0] + x[1] * a[1] + x[2] * a[2]


def unrolled(count, step, body):
    def trip(t, carry):
        for u in range(step):
            body(t * step + u)
        return carry

    lax.fori_loop(0, count // step, trip, 0)


def split2(value):
    high = value.astype(bf16)
    return high, (value - high.astype(f32)).astype(bf16)


def fill_bases(tiles, bases):
    bases[...] = tiles[...]

    def group(t):
        x, a = [[tiles[pl.ds(t * 64 + first + k, 8, stride=8), :] for k in range(3)] for first in (0, 3)]
        for k, row in enumerate(cross_rows(x, a)):
            bases[pl.ds(t * 64 + k, 8, stride=8), :] = row

    unrolled(tiles.shape[0] // 64, 2, group)


def features(tile, base):
    x = [tile[k : k + 1] for k in range(3)]
    parts = []
    for scale in (None, x[0], x[1], x[2]):
        value = base if scale is None else scale * base
        high = value.astype(bf16).astype(f32)
        rest = value - high
        middle = rest.astype(bf16).astype(f32)
        parts += [high, middle, rest - middle]
        if scale is None:
            parts.append(jnp.zeros((8, 128), f32))
    return jnp.concatenate(parts + [jnp.zeros((8, 128), f32)], axis=0).astype(bf16)


def columns(tile):
    flipped = jnp.concatenate([tile] * 16, axis=0).T
    return [jnp.broadcast_to(flipped[:, k : k + 1], (128, 128)) for k in range(3)]


def weights(cols, tile, skip=None):
    d = [cols[k] - tile[k : k + 1] for k in range(3)]
    soft = dot_rows(d, d) + sigma_sq
    inverse = lax.rsqrt(soft)
    square = inverse * inverse
    cubic = square * inverse
    quintic = square * cubic
    smooth = jnp.exp2(soft * smooth_rate)
    if skip is not None:
        quintic, cubic, smooth = [jnp.where(skip, 0.0, value) for value in (quintic, cubic, smooth)]
    return split2(quintic), split2(cubic), (smooth.astype(bf16),)


def moments(wide, mats, dims):
    twice = jnp.concatenate([wide, wide], axis=1)
    out = []
    for parts, left in zip(mats, (twice, twice[0:32], wide[0:32])):
        right = jnp.concatenate(parts, axis=1 if dims is NT else 0) if len(parts) > 1 else parts[0]
        sums = lax.dot_general(left, right, dims, preferred_element_type=f32)
        starts = (0, 32, 56, 80) if left.shape[0] > 32 else (0,)
        out += [sums[k : k + 8] + sums[k + 8 : k + 16] + sums[k + 16 : k + 24] for k in starts]
    return out


def put(target, c, tiles, add=False):
    for k, tile in enumerate(tiles):
        rows = pl.ds(pl.multiple_of(c * MOMENTS + 8 * k, 8), 8)
        target[rows, :] = target[rows, :] + tile if add else tile


def credits(tiles, moment, out):
    def group(t):
        def cell_rows(first, count=3):
            return [tiles[pl.ds(t * 64 + first + k, 8, stride=8), :] for k in range(count)]

        def sums(which, first, count=3):
            at = t * 8 * MOMENTS + which * 8 + first
            return [moment[pl.ds(at + k, 8, stride=MOMENTS), :] for k in range(count)]

        x, a = cell_rows(0), cell_rows(3)
        spin = dot_rows(a, x)
        parts = [sums(which, 0, 6) for which in range(5)]
        mixed = [
            spin * parts[0][r] - a[0] * parts[1][r] - a[1] * parts[2][r] - a[2] * parts[3][r] for r in range(6)
        ]
        cubic = parts[4]
        turn, drift = cross_rows(x, mixed[3:6]), cross_rows(x, cubic[3:6])
        twist = cross_rows(a, cubic[3:6])
        spread, total = sums(5, 3), sums(5, 6, 1)[0]
        for k in range(3):
            out[pl.ds(t * 64 + k, 8, stride=8), :] = -kernel_scale * (drift[k] - cubic[k])
            out[pl.ds(t * 64 + 3 + k, 8, stride=8), :] = -kernel_scale * (
                twist[k] - 3.0 * (turn[k] - mixed[k])
            ) + smooth_scale * (spread[k] - a[k] * total)
        for k in (6, 7):
            out[pl.ds(t * 64 + k, 8, stride=8), :] = jnp.zeros((8, 128), f32)

    unrolled(tiles.shape[0] // 64, 2, group)


def tile_rows(ref, c):
    return ref[pl.ds(pl.multiple_of(c * 8, 8), 8), :]


def pack_kernel(fill, exports, places_ref, vortices_ref, cells_ref, sent_ref, places, vortices, sems):
    copies = [
        pltpu.make_async_copy(source.at[0], kept, sems.at[0, k])
        for k, (source, kept) in enumerate(((places_ref, places), (vortices_ref, vortices)))
    ]
    for copy in copies:
        copy.start()
    for copy in copies:
        copy.wait()
    lane = lax.broadcasted_iota(jnp.int32, (1, 128), 1)
    for c in range(cells_ref.shape[0] // 8):
        mask = (lane < fill[c]).astype(f32)
        rows = [places[k, c : c + 1] - 1.0 for k in range(3)]
        rows += [vortices[k, c : c + 1] * mask for k in range(3)]
        cells_ref[8 * c : 8 * c + 8] = jnp.concatenate(rows + [mask, jnp.zeros((1, 128), f32)], axis=0)
    send(exports, cells_ref, sent_ref)


def send(exports, cells_ref, sent_ref):
    def one(n):
        sent_ref[pl.ds(pl.multiple_of(n * 8, 8), 8), :] = tile_rows(cells_ref, exports[n])

    unrolled(sent_ref.shape[0] // 8, 8, one)


def near_kernel(
    cells_ref, above_ref, near_ref, far_ref, wide_out, cols_out,
    base_here, base_there, mom_near, mom_far, wide_here, cols_here, sems,
):
    fill_bases(cells_ref, base_here)
    fill_bases(above_ref, base_there)
    row, column = [lax.broadcasted_iota(jnp.int32, (128, 128), axis) for axis in (0, 1)]
    itself = row == column

    def cell(c):
        here, there = tile_rows(cells_ref, c), tile_rows(above_ref, c)
        wide = features(here, tile_rows(base_here, c))
        wide_there = features(there, tile_rows(base_there, c))
        cols = columns(here)
        joint = weights(cols, there)
        near = moments(wide_there, joint, NT)
        far = moments(wide, joint, NN)
        own = moments(wide, weights(cols, here, itself), NN)
        wide_here[c, 0] = wide
        for k in range(3):
            cols_here[c, k] = cols[k]
        put(mom_far, c, far)
        put(mom_near, c, [p + q for p, q in zip(near, own)])

    half = wide_here.shape[0] // 2
    copies = []
    for part in range(2):
        unrolled(half, 4, lambda c: cell(c + part * half))
        rows = pl.ds(part * half, half)
        for k, (kept, out) in enumerate(((wide_here, wide_out), (cols_here, cols_out))):
            copies.append(pltpu.make_async_copy(kept.at[rows], out.at[rows], sems.at[part, k]))
            copies[-1].start()
    credits(above_ref, mom_far, far_ref)
    credits(cells_ref, mom_near, near_ref)
    for copy in copies:
        copy.wait()


def far_kernel(
    here_ids, there_ids, count, wide_ref, cols_ref, got_ref, far_ref, wide_out, begun_ref,
    wide_here, cols, sems, base, mom, mom_here,
):
    cells, imports = cols.shape[0], wide_out.shape[0]
    copies = [
        pltpu.make_async_copy(source, kept, sems.at[0, k])
        for k, (source, kept) in enumerate(((wide_ref, wide_here), (cols_ref, cols)))
    ]
    for copy in copies:
        copy.start()
    fill_bases(got_ref, base)
    mom[...] = jnp.zeros(mom.shape, f32)
    mom_here[...] = jnp.zeros(mom_here.shape, f32)

    def prepare(b):
        wide_out[b] = features(tile_rows(got_ref, b), tile_rows(base, b))

    unrolled(imports, 8, prepare)
    for copy in copies:
        copy.wait()

    def pair(n, both):
        c, b = here_ids[n], there_ids[n]
        cell, source = jnp.minimum(c, cells - 1), jnp.minimum(b, imports - 1)
        mats = weights([cols[cell, k] for k in range(3)], tile_rows(got_ref, source))
        put(mom, b, moments(wide_here[cell, 0], mats, NN), add=True)
        if both:
            put(mom_here, c, moments(wide_out[source], mats, NT), add=True)

    joint, total = trips(count)
    pairs(0, joint, lambda n: pair(n, True))
    begun = pltpu.make_async_copy(mom_here, begun_ref, sems.at[1, 0])
    begun.start()
    pairs(joint, total, lambda n: pair(n, False))
    credits(got_ref, mom, far_ref)
    begun.wait()


def here_kernel(here_ids, there_ids, count, cols_ref, wide_ref, got_ref, cells_ref, begun_ref, own_ref, cols, sems, mom):
    cells, imports = cols.shape[0], wide_ref.shape[0]
    copies = [
        pltpu.make_async_copy(source, kept, sems.at[0, k])
        for k, (source, kept) in enumerate(((cols_ref, cols), (begun_ref, mom)))
    ]
    for copy in copies:
        copy.start()
    for copy in copies:
        copy.wait()

    def pair(n):
        c, b = here_ids[n], jnp.minimum(there_ids[n], imports - 1)
        cell = jnp.minimum(c, cells - 1)
        mats = weights([cols[cell, k] for k in range(3)], tile_rows(got_ref, b))
        put(mom, c, moments(wide_ref[b], mats, NT), add=True)

    pairs(*trips(count), pair)
    credits(cells_ref, mom, own_ref)


def trips(count):
    total = (count[0] + UNROLL - 1) // UNROLL
    return jnp.maximum(total - HIDDEN, 0), total


def pairs(first, last, pair):
    def trip(t, carry):
        for u in range(UNROLL):
            pair(t * UNROLL + u)
        return carry

    lax.fori_loop(first, last, trip, 0)


def gather_rates(exports, cells_ref, parts, back_ref, total_ref):
    total_ref[...] = parts[0][...] + parts[1][...] + parts[2][...]

    def add(n):
        at = pl.ds(pl.multiple_of(exports[n] * 8, 8), 8)
        total_ref[at, :] = total_ref[at, :] + tile_rows(back_ref, n)

    unrolled(back_ref.shape[0] // 8, 8, add)
    for c in range(total_ref.shape[0] // 8):
        rows = slice(8 * c, 8 * c + 8)
        total_ref[rows] = total_ref[rows] * cells_ref[8 * c + 6 : 8 * c + 7]


def middle_kernel(exports, cells_ref, near, remote, below, back_ref, first_ref, mid_ref, sent_ref):
    gather_rates(exports, cells_ref, (near, remote, below), back_ref, first_ref)
    mid_ref[...] = cells_ref[...] + time_step * first_ref[...]
    send(exports, mid_ref, sent_ref)


def last_kernel(
    exports, cells_ref, near, remote, below, back_ref, first_ref, places, vortices,
    new_places, new_vortices, total_ref,
):
    gather_rates(exports, cells_ref, (near, remote, below), back_ref, total_ref)
    half = 0.5 * time_step
    for c in range(total_ref.shape[0] // 8):
        change = half * (first_ref[8 * c : 8 * c + 8] + total_ref[8 * c : 8 * c + 8])
        for k in range(3):
            new_places[k, c : c + 1] = places[k, c : c + 1] + change[k : k + 1]
            new_vortices[k, c : c + 1] = vortices[k, c : c + 1] + change[3 + k : 4 + k]


def call(body, scalars, arrays, outs, scratch=(), name=None, held=()):
    def stays(shape):
        return len(shape) == 4 or shape in held

    def spec(one):
        if stays(one.shape):
            return pl.BlockSpec(memory_space=pltpu.HBM)
        zeros = (0,) * len(one.shape)
        return pl.BlockSpec(one.shape, lambda i, *_: zeros, pipeline_mode=pl.Buffered(1))

    outs = [out if len(out) == 2 and isinstance(out[0], tuple) else (out, f32) for out in outs]
    outs = [pltpu.HBM(*out) if stays(out[0]) else jax.ShapeDtypeStruct(*out) for out in outs]
    arrays = [pltpu.with_memory_space_constraint(one, pltpu.HBM) if stays(one.shape) else one for one in arrays]
    return pl.pallas_call(
        body,
        grid_spec=pltpu.PrefetchScalarGridSpec(
            num_scalar_prefetch=len(scalars),
            grid=(1,),
            in_specs=[spec(array) for array in arrays],
            out_specs=[spec(out) for out in outs],
            scratch_shapes=[pltpu.VMEM(one, f32) if isinstance(one, tuple) else one for one in scratch],
        ),
        out_shape=outs,
        compiler_params=pltpu.CompilerParams(vmem_limit_bytes=20 << 20),
        cost_estimate=pl.CostEstimate(flops=10**10 if name in ("near", "far", "here") else 10**8, bytes_accessed=10**6, transcendentals=0),
        name=name,
    )(*scalars, *arrays)


def local(positions, strengths, fill, export_cells, pair_local, pair_remote, pair_count):
    places = jnp.transpose(positions[0], (1, 0, 2))
    vortices = jnp.transpose(strengths[0], (1, 0, 2))
    cells = places.shape[1]
    owners, per_owner = export_cells.shape[2:]
    imports = owners * per_owner
    exports = export_cells[0, 0].reshape(-1)
    count = pair_count[0]
    alive = jnp.arange(pair_local.shape[1], dtype=jnp.int32) < count
    here_ids = jnp.where(alive, pair_local[0], cells)
    there_ids = jnp.where(alive, pair_remote[0], imports)
    tile, traded = (cells * 8, 128), (imports * 8, 128)
    spread, gathered = (cells, 3, 128, 128), ((cells + 1) * MOMENTS, 128)
    kept, sems = pltpu.VMEM((cells, 1, 112, 128), bf16), pltpu.SemaphoreType.DMA((2, 2))

    def exchange(value):
        value = value.reshape(owners, per_owner, 8, 128)
        value = lax.all_to_all(value, "cell", split_axis=0, concat_axis=0, tiled=True)
        return value.reshape(traded)

    def rates(packed, sent):
        above = shifted(packed, "stream", 1)
        got = exchange(sent)
        near, far, wide, cols = call(
            near_kernel, (), (packed, above), (tile, tile, ((cells, 1, 112, 128), bf16), spread),
            (tile, tile, (cells * MOMENTS, 128), (cells * MOMENTS, 128), kept, spread, sems), name="near",
        )
        below = shifted(far, "stream", -1)
        got, near = lax.optimization_barrier((got, near))
        listed = (here_ids, there_ids, count)
        back, wide_there, begun = call(
            far_kernel, listed, (wide, cols, got), (traded, ((imports, 112, 128), bf16), gathered),
            (kept, spread, sems, traded, ((imports + 1) * MOMENTS, 128), gathered), name="far", held=(gathered,),
        )
        returned = exchange(back)
        (remote,) = call(
            here_kernel, listed, (cols, wide_there, got, packed, begun), (tile,),
            (spread, sems, gathered), name="here", held=(gathered,),
        )
        return near, remote, below, returned

    packed, sent = call(pack_kernel, (fill[0], exports), (places[None], vortices[None]), (tile, traded), (places.shape, places.shape, sems), name="pack")
    first, middle, sent = call(
        middle_kernel, (exports,), (packed, *rates(packed, sent)), (tile, tile, traded), name="middle"
    )
    shape = places.shape
    new_places, new_vortices = call(
        last_kernel, (exports,), (middle, *rates(middle, sent), first, places, vortices), (shape, shape),
        (tile,), name="last",
    )
    return (jnp.transpose(new_places, (1, 0, 2))[None], jnp.transpose(new_vortices, (1, 0, 2))[None])


def solution(mesh):
    in_specs = (
        P("stream", "cell", None, None),
        P("stream", "cell", None, None),
        P("stream", "cell"),
        P("stream", "cell", None, None),
        P("stream", "cell"),
        P("stream", "cell"),
        P("stream", "cell"),
    )
    out_specs = (P("stream", "cell", None, None), P("stream", "cell", None, None))
    return jax.shard_map(local, mesh=mesh, in_specs=in_specs, out_specs=out_specs, check_vma=False)
```

```python
import math

import jax
import jax.numpy as jnp
from jax import lax
from jax.experimental import pallas as pl
from jax.experimental.pallas import tpu as pltpu
from jax.sharding import PartitionSpec as P

sigma_sq = 0.09
spread_inv = 3.125
viscous = 0.01
time_step = 0.2
kernel_scale = 1.0 / (4.0 * math.pi)
smooth_rate = -spread_inv * math.log2(math.e)
smooth_scale = viscous * math.exp(spread_inv * sigma_sq)

f32 = jnp.float32
bf16 = jnp.bfloat16
MOMENTS = 48
UNROLL = 32
HIDDEN = 4
NN = (((1,), (0,)), ((), ()))
NT = (((1,), (1,)), ((), ()))


def shifted(value, axis, steps):
    count = lax.axis_size(axis)
    leading, last = (max(0, -steps), min(count, count - steps))
    return lax.ppermute(value, axis, [(source, source + steps) for source in range(leading, last)])


def cross_rows(x, a):
    return [
        x[1] * a[2] - x[2] * a[1],
        x[2] * a[0] - x[0] * a[2],
        x[0] * a[1] - x[1] * a[0],
    ]


def dot_rows(x, a):
    return x[0] * a[0] + x[1] * a[1] + x[2] * a[2]


def unrolled(count, step, body):
    def trip(t, carry):
        for u in range(step):
            body(t * step + u)
        return carry

    lax.fori_loop(0, count // step, trip, 0)


def split2(value):
    high = value.astype(bf16)
    return high, (value - high.astype(f32)).astype(bf16)


def fill_bases(tiles, bases):
    bases[...] = tiles[...]

    def group(t):
        x, a = [[tiles[pl.ds(t * 64 + first + k, 8, stride=8), :] for k in range(3)] for first in (0, 3)]
        for k, row in enumerate(cross_rows(x, a)):
            bases[pl.ds(t * 64 + k, 8, stride=8), :] = row

    unrolled(tiles.shape[0] // 64, 2, group)


def features(tile, base):
    x = [tile[k : k + 1] for k in range(3)]
    parts = []
    for scale in (None, x[0], x[1], x[2]):
        value = base if scale is None else scale * base
        high = value.astype(bf16).astype(f32)
        rest = value - high
        middle = rest.astype(bf16).astype(f32)
        parts += [high, middle, rest - middle]
        if scale is None:
            parts.append(jnp.zeros((8, 128), f32))
    return jnp.concatenate(parts + [jnp.zeros((8, 128), f32)], axis=0).astype(bf16)


def columns(tile):
    flipped = jnp.concatenate([tile] * 16, axis=0).T
    return [jnp.broadcast_to(flipped[:, k : k + 1], (128, 128)) for k in range(3)]


def weights(cols, tile, skip=None):
    d = [cols[k] - tile[k : k + 1] for k in range(3)]
    soft = dot_rows(d, d) + sigma_sq
    inverse = lax.rsqrt(soft)
    square = inverse * inverse
    cubic = square * inverse
    quintic = square * cubic
    smooth = jnp.exp2(soft * smooth_rate)
    if skip is not None:
        quintic, cubic, smooth = [jnp.where(skip, 0.0, value) for value in (quintic, cubic, smooth)]
    return split2(quintic), split2(cubic), (smooth.astype(bf16),)


def moments(wide, mats, dims):
    twice = jnp.concatenate([wide, wide], axis=1)
    out = []
    for parts, left in zip(mats, (twice, twice[0:32], wide[0:32])):
        right = jnp.concatenate(parts, axis=1 if dims is NT else 0) if len(parts) > 1 else parts[0]
        sums = lax.dot_general(left, right, dims, preferred_element_type=f32)
        starts = (0, 32, 56, 80) if left.shape[0] > 32 else (0,)
        out += [sums[k : k + 8] + sums[k + 8 : k + 16] + sums[k + 16 : k + 24] for k in starts]
    return out


def put(target, c, tiles, add=False):
    for k, tile in enumerate(tiles):
        rows = pl.ds(pl.multiple_of(c * MOMENTS + 8 * k, 8), 8)
        target[rows, :] = target[rows, :] + tile if add else tile


def credits(tiles, moment, out):
    def group(t):
        def cell_rows(first, count=3):
            return [tiles[pl.ds(t * 64 + first + k, 8, stride=8), :] for k in range(count)]

        def sums(which, first, count=3):
            at = t * 8 * MOMENTS + which * 8 + first
            return [moment[pl.ds(at + k, 8, stride=MOMENTS), :] for k in range(count)]

        x, a = cell_rows(0), cell_rows(3)
        spin = dot_rows(a, x)
        parts = [sums(which, 0, 6) for which in range(5)]
        mixed = [
            spin * parts[0][r] - a[0] * parts[1][r] - a[1] * parts[2][r] - a[2] * parts[3][r] for r in range(6)
        ]
        cubic = parts[4]
        turn, drift = cross_rows(x, mixed[3:6]), cross_rows(x, cubic[3:6])
        twist = cross_rows(a, cubic[3:6])
        spread, total = sums(5, 3), sums(5, 6, 1)[0]
        for k in range(3):
            out[pl.ds(t * 64 + k, 8, stride=8), :] = -kernel_scale * (drift[k] - cubic[k])
            out[pl.ds(t * 64 + 3 + k, 8, stride=8), :] = -kernel_scale * (
                twist[k] - 3.0 * (turn[k] - mixed[k])
            ) + smooth_scale * (spread[k] - a[k] * total)
        for k in (6, 7):
            out[pl.ds(t * 64 + k, 8, stride=8), :] = jnp.zeros((8, 128), f32)

    unrolled(tiles.shape[0] // 64, 2, group)


def tile_rows(ref, c):
    return ref[pl.ds(pl.multiple_of(c * 8, 8), 8), :]


def pack_kernel(fill, exports, places_ref, vortices_ref, cells_ref, sent_ref, places, vortices, sems):
    copies = [
        pltpu.make_async_copy(source.at[0], kept, sems.at[0, k])
        for k, (source, kept) in enumerate(((places_ref, places), (vortices_ref, vortices)))
    ]
    for copy in copies:
        copy.start()
    for copy in copies:
        copy.wait()
    lane = lax.broadcasted_iota(jnp.int32, (1, 128), 1)
    for c in range(cells_ref.shape[0] // 8):
        mask = (lane < fill[c]).astype(f32)
        rows = [places[k, c : c + 1] - 1.0 for k in range(3)]
        rows += [vortices[k, c : c + 1] * mask for k in range(3)]
        cells_ref[8 * c : 8 * c + 8] = jnp.concatenate(rows + [mask, jnp.zeros((1, 128), f32)], axis=0)
    send(exports, cells_ref, sent_ref)


def send(exports, cells_ref, sent_ref):
    def one(n):
        sent_ref[pl.ds(pl.multiple_of(n * 8, 8), 8), :] = tile_rows(cells_ref, exports[n])

    unrolled(sent_ref.shape[0] // 8, 8, one)


def near_kernel(
    cells_ref, above_ref, near_ref, far_ref, wide_out, cols_out,
    base_here, base_there, mom_near, mom_far, wide_here, cols_here, sems,
):
    fill_bases(cells_ref, base_here)
    fill_bases(above_ref, base_there)
    row, column = [lax.broadcasted_iota(jnp.int32, (128, 128), axis) for axis in (0, 1)]
    itself = row == column

    def cell(c):
        here, there = tile_rows(cells_ref, c), tile_rows(above_ref, c)
        wide = features(here, tile_rows(base_here, c))
        wide_there = features(there, tile_rows(base_there, c))
        cols = columns(here)
        joint = weights(cols, there)
        near = moments(wide_there, joint, NT)
        far = moments(wide, joint, NN)
        own = moments(wide, weights(cols, here, itself), NN)
        wide_here[c, 0] = wide
        for k in range(3):
            cols_here[c, k] = cols[k]
        put(mom_far, c, far)
        put(mom_near, c, [p + q for p, q in zip(near, own)])

    half = wide_here.shape[0] // 2
    copies = []
    for part in range(2):
        unrolled(half, 8, lambda c: cell(c + part * half))
        rows = pl.ds(part * half, half)
        for k, (kept, out) in enumerate(((wide_here, wide_out), (cols_here, cols_out))):
            copies.append(pltpu.make_async_copy(kept.at[rows], out.at[rows], sems.at[part, k]))
            copies[-1].start()
    credits(above_ref, mom_far, far_ref)
    credits(cells_ref, mom_near, near_ref)
    for copy in copies:
        copy.wait()


def far_kernel(
    here_ids, there_ids, count, wide_ref, cols_ref, got_ref, far_ref, wide_out, begun_ref,
    wide_here, cols, sems, base, mom, mom_here,
):
    cells, imports = cols.shape[0], wide_out.shape[0]
    copies = [
        pltpu.make_async_copy(source, kept, sems.at[0, k])
        for k, (source, kept) in enumerate(((wide_ref, wide_here), (cols_ref, cols)))
    ]
    for copy in copies:
        copy.start()
    fill_bases(got_ref, base)
    mom[...] = jnp.zeros(mom.shape, f32)
    mom_here[...] = jnp.zeros(mom_here.shape, f32)

    def prepare(b):
        wide_out[b] = features(tile_rows(got_ref, b), tile_rows(base, b))

    unrolled(imports, 8, prepare)
    for copy in copies:
        copy.wait()

    def pair(n, both):
        c, b = here_ids[n], there_ids[n]
        cell, source = jnp.minimum(c, cells - 1), jnp.minimum(b, imports - 1)
        mats = weights([cols[cell, k] for k in range(3)], tile_rows(got_ref, source))
        put(mom, b, moments(wide_here[cell, 0], mats, NN), add=True)
        if both:
            put(mom_here, c, moments(wide_out[source], mats, NT), add=True)

    joint, total = trips(count)
    pairs(0, joint, lambda n: pair(n, True))
    begun = pltpu.make_async_copy(mom_here, begun_ref, sems.at[1, 0])
    begun.start()
    pairs(joint, total, lambda n: pair(n, False))
    credits(got_ref, mom, far_ref)
    begun.wait()


def here_kernel(here_ids, there_ids, count, cols_ref, wide_ref, got_ref, cells_ref, begun_ref, own_ref, cols, sems, mom):
    cells, imports = cols.shape[0], wide_ref.shape[0]
    copies = [
        pltpu.make_async_copy(source, kept, sems.at[0, k])
        for k, (source, kept) in enumerate(((cols_ref, cols), (begun_ref, mom)))
    ]
    for copy in copies:
        copy.start()
    for copy in copies:
        copy.wait()

    def pair(n):
        c, b = here_ids[n], jnp.minimum(there_ids[n], imports - 1)
        cell = jnp.minimum(c, cells - 1)
        mats = weights([cols[cell, k] for k in range(3)], tile_rows(got_ref, b))
        put(mom, c, moments(wide_ref[b], mats, NT), add=True)

    pairs(*trips(count), pair)
    credits(cells_ref, mom, own_ref)


def trips(count):
    total = (count[0] + UNROLL - 1) // UNROLL
    return jnp.maximum(total - HIDDEN, 0), total


def pairs(first, last, pair):
    def trip(t, carry):
        for u in range(UNROLL):
            pair(t * UNROLL + u)
        return carry

    lax.fori_loop(first, last, trip, 0)


def gather_rates(exports, cells_ref, parts, back_ref, total_ref):
    total_ref[...] = parts[0][...] + parts[1][...] + parts[2][...]

    def add(n):
        at = pl.ds(pl.multiple_of(exports[n] * 8, 8), 8)
        total_ref[at, :] = total_ref[at, :] + tile_rows(back_ref, n)

    unrolled(back_ref.shape[0] // 8, 8, add)
    for c in range(total_ref.shape[0] // 8):
        rows = slice(8 * c, 8 * c + 8)
        total_ref[rows] = total_ref[rows] * cells_ref[8 * c + 6 : 8 * c + 7]


def middle_kernel(exports, cells_ref, near, remote, below, back_ref, first_ref, mid_ref, sent_ref):
    gather_rates(exports, cells_ref, (near, remote, below), back_ref, first_ref)
    mid_ref[...] = cells_ref[...] + time_step * first_ref[...]
    send(exports, mid_ref, sent_ref)


def last_kernel(
    exports, cells_ref, near, remote, below, back_ref, first_ref, places, vortices,
    new_places, new_vortices, total_ref,
):
    gather_rates(exports, cells_ref, (near, remote, below), back_ref, total_ref)
    half = 0.5 * time_step
    for c in range(total_ref.shape[0] // 8):
        change = half * (first_ref[8 * c : 8 * c + 8] + total_ref[8 * c : 8 * c + 8])
        for k in range(3):
            new_places[k, c : c + 1] = places[k, c : c + 1] + change[k : k + 1]
            new_vortices[k, c : c + 1] = vortices[k, c : c + 1] + change[3 + k : 4 + k]


def call(body, scalars, arrays, outs, scratch=(), name=None, held=()):
    def stays(shape):
        return len(shape) == 4 or shape in held

    def spec(one):
        if stays(one.shape):
            return pl.BlockSpec(memory_space=pltpu.HBM)
        zeros = (0,) * len(one.shape)
        return pl.BlockSpec(one.shape, lambda i, *_: zeros, pipeline_mode=pl.Buffered(1))

    outs = [out if len(out) == 2 and isinstance(out[0], tuple) else (out, f32) for out in outs]
    outs = [pltpu.HBM(*out) if stays(out[0]) else jax.ShapeDtypeStruct(*out) for out in outs]
    arrays = [pltpu.with_memory_space_constraint(one, pltpu.HBM) if stays(one.shape) else one for one in arrays]
    return pl.pallas_call(
        body,
        grid_spec=pltpu.PrefetchScalarGridSpec(
            num_scalar_prefetch=len(scalars),
            grid=(1,),
            in_specs=[spec(array) for array in arrays],
            out_specs=[spec(out) for out in outs],
            scratch_shapes=[pltpu.VMEM(one, f32) if isinstance(one, tuple) else one for one in scratch],
        ),
        out_shape=outs,
        compiler_params=pltpu.CompilerParams(vmem_limit_bytes=20 << 20),
        cost_estimate=pl.CostEstimate(flops=10**10 if name in ("near", "far", "here") else 10**8, bytes_accessed=10**6, transcendentals=0),
        name=name,
    )(*scalars, *arrays)


def local(positions, strengths, fill, export_cells, pair_local, pair_remote, pair_count):
    places = jnp.transpose(positions[0], (1, 0, 2))
    vortices = jnp.transpose(strengths[0], (1, 0, 2))
    cells = places.shape[1]
    owners, per_owner = export_cells.shape[2:]
    imports = owners * per_owner
    exports = export_cells[0, 0].reshape(-1)
    count = pair_count[0]
    alive = jnp.arange(pair_local.shape[1], dtype=jnp.int32) < count
    here_ids = jnp.where(alive, pair_local[0], cells)
    there_ids = jnp.where(alive, pair_remote[0], imports)
    tile, traded = (cells * 8, 128), (imports * 8, 128)
    spread, gathered = (cells, 3, 128, 128), ((cells + 1) * MOMENTS, 128)
    kept, sems = pltpu.VMEM((cells, 1, 112, 128), bf16), pltpu.SemaphoreType.DMA((2, 2))

    def exchange(value):
        value = value.reshape(owners, per_owner, 8, 128)
        value = lax.all_to_all(value, "cell", split_axis=0, concat_axis=0, tiled=True)
        return value.reshape(traded)

    def rates(packed, sent):
        above = shifted(packed, "stream", 1)
        got = exchange(sent)
        near, far, wide, cols = call(
            near_kernel, (), (packed, above), (tile, tile, ((cells, 1, 112, 128), bf16), spread),
            (tile, tile, (cells * MOMENTS, 128), (cells * MOMENTS, 128), kept, spread, sems), name="near",
        )
        below = shifted(far, "stream", -1)
        got, near = lax.optimization_barrier((got, near))
        listed = (here_ids, there_ids, count)
        back, wide_there, begun = call(
            far_kernel, listed, (wide, cols, got), (traded, ((imports, 112, 128), bf16), gathered),
            (kept, spread, sems, traded, ((imports + 1) * MOMENTS, 128), gathered), name="far", held=(gathered,),
        )
        returned = exchange(back)
        (remote,) = call(
            here_kernel, listed, (cols, wide_there, got, packed, begun), (tile,),
            (spread, sems, gathered), name="here", held=(gathered,),
        )
        return near, remote, below, returned

    packed, sent = call(pack_kernel, (fill[0], exports), (places[None], vortices[None]), (tile, traded), (places.shape, places.shape, sems), name="pack")
    first, middle, sent = call(
        middle_kernel, (exports,), (packed, *rates(packed, sent)), (tile, tile, traded), name="middle"
    )
    shape = places.shape
    new_places, new_vortices = call(
        last_kernel, (exports,), (middle, *rates(middle, sent), first, places, vortices), (shape, shape),
        (tile,), name="last",
    )
    return (jnp.transpose(new_places, (1, 0, 2))[None], jnp.transpose(new_vortices, (1, 0, 2))[None])


def solution(mesh):
    in_specs = (
        P("stream", "cell", None, None),
        P("stream", "cell", None, None),
        P("stream", "cell"),
        P("stream", "cell", None, None),
        P("stream", "cell"),
        P("stream", "cell"),
        P("stream", "cell"),
    )
    out_specs = (P("stream", "cell", None, None), P("stream", "cell", None, None))
    return jax.shard_map(local, mesh=mesh, in_specs=in_specs, out_specs=out_specs, check_vma=False)
```
